512 devices in a mesh: dom: 8 (over y, z_hi), gz: 64 (over z_lo, x, core).
Axes of the slice: x: 4, y: 4, z: 16 (z_hi: 2, z_lo: 8; z = z_hi * 8 + z_lo), core: 2. Of those that a mesh axis runs over, the one named last changes fastest.
Arguments:
- velocity: bfloat16 [8, 3, 128, 512, 256], P('dom', None, 'gz'), may hold values from -2.5 to 3.9
- eddy_viscosity: float32 [128], replicated, may hold values from 0.03 to 0.15
- cell_height: float32 [128], replicated, may hold values from 0.5 to 2
- z_vectors: float32 [128, 128], replicated, as said below
- z_inverse: float32 [128, 128], replicated, as said below
- z_values: float32 [128], replicated, may hold values from 0 to 24, as said below
- feed_source: int32 [8, 3], replicated, may hold values from 0 to 7, as said below
- fringe_strength: float32 [8], replicated, may hold values from 0.3 to 0.95
- fringe_start: int32 [1], replicated, may hold values from 0 to 480
- turbines: int32 [8, 8, 5], replicated, may hold values from 0 to 512, as said below
- thrust: float32 [8, 8], replicated, may hold values from 0.3 to 0.9
Outputs:
- corrected_velocity: bfloat16 [8, 3, 128, 512, 256], P('dom', None, 'gz')
The draws below stay inside these ranges and needn't reach their ends.
Inputs may be any that keep to these rules, and one draw needn't show every extreme that they name: z_vectors diag(z_values) z_inverse is, up to rounding, the operator that maps a column p to minus (g[z] - g[z-1]) / cell_height[z], g[z] = (p[z+1] - p[z]) / ((cell_height[z] + cell_height[z+1]) / 2), g[-1] = 0, p[128] = 0, cell_height[128] = 0; z_inverse is the inverse of z_vectors. `z_inverse`: the inverse of z_vectors, up to rounding. `z_values`: all positive. `feed_source`: in every row at least one component is fed by a domain other than the row's own. `turbines`: each row (c, ya, yb, za, zb) has c < 512, ya < yb <= 256, za < zb <= 128, and both yb - ya and zb - za between 6 and 12.
All inputs are finite; a program needn't handle non-finite values.
Results may differ from the reference program's by a relative error of at most 0.0004.
Values may be sent and summed in bfloat16 or wider, within the bound.
No kernel may reach another device: no remote copies, remote signals or barrier semaphores. Data moves between devices by JAX's collectives and lax.ppermute only.
A program may use at most 64 MiB of HBM per device.

```python
import math
import jax
import jax.numpy as jnp
from jax import lax

NX = 512
NY = 256
NZ = 128
FRINGE = 32
TURBINES = 8
DISC = 12
DOMAINS = 8


def vertical_factors(key):
    inner = jax.random.fold_in(key, 41)
    heights = jnp.exp(jax.random.uniform(inner, (NZ,), jnp.float32, jnp.log(0.5), jnp.log(2.0)))
    next_height = jnp.concatenate([heights[1:], jnp.zeros((1,), jnp.float32)])
    half_gap = 0.5 * (heights + next_height)
    coupling = 1.0 / half_gap
    lower_coupling = jnp.concatenate([jnp.zeros((1,), jnp.float32), coupling[:-1]])
    stiffness = jnp.diag(coupling + lower_coupling) - jnp.diag(coupling[:-1], 1) - jnp.diag(coupling[:-1], -1)
    scaling = 1.0 / jnp.sqrt(heights)
    symmetric = scaling[:, None] * stiffness * scaling[None, :]
    eigen_values, basis = jnp.linalg.eigh(symmetric)
    vectors = scaling[:, None] * basis
    inverse = basis.T / scaling[None, :]
    return (heights, vectors, inverse, eigen_values)


def draw_cell_height(key, part):
    return vertical_factors(key)[0].astype(jnp.float32)


def draw_z_vectors(key, part):
    return vertical_factors(key)[1].astype(jnp.float32)


def draw_z_inverse(key, part):
    return vertical_factors(key)[2].astype(jnp.float32)


def draw_z_values(key, part):
    return vertical_factors(key)[3].astype(jnp.float32)


def draw_feed_source(key, part):
    value_key, pick_key, step_key = jax.random.split(jax.random.fold_in(key, 17), 3)
    values = jax.random.randint(value_key, (DOMAINS, 3), 0, DOMAINS)
    picked = jax.random.randint(pick_key, (DOMAINS,), 0, 3)
    steps = jax.random.randint(step_key, (DOMAINS,), 1, DOMAINS)
    others = (jnp.arange(DOMAINS, dtype=jnp.int32) + steps) % DOMAINS
    selected = jnp.arange(3, dtype=jnp.int32)[None, :] == picked[:, None]
    return jnp.where(selected, others[:, None], values).astype(jnp.int32)


def draw_velocity(key, part):
    inflow_random_key, jitter_key = jax.random.split(jax.random.fold_in(key, 3))
    average_inflow = jax.random.uniform(inflow_random_key, (DOMAINS, 1, NZ, 1, 1), jnp.float32, 0.6, 1.4)
    random_perturbation = 0.5 * jax.random.normal(jitter_key, (DOMAINS, 3, NZ, NX, NY), jnp.float32)
    random_perturbation = jnp.clip(random_perturbation, -2.5, 2.5)
    relay_buffer = (jnp.arange(3) == 0).astype(jnp.float32)[None, :, None, None, None]
    return (random_perturbation + relay_buffer * average_inflow).astype(jnp.bfloat16)


def draw_turbines(key, part):
    streams = jax.random.split(jax.random.fold_in(key, 9), 5)
    layout = (DOMAINS, TURBINES)
    column_x = jax.random.randint(streams[0], layout, 0, NX)
    extent_y = jax.random.randint(streams[1], layout, DISC // 2, DISC + 1)
    lowest_y = jax.random.randint(streams[2], layout, 0, NY - extent_y + 1)
    extent_z = jax.random.randint(streams[3], layout, DISC // 2, DISC + 1)
    lowest_z = jax.random.randint(streams[4], layout, 0, NZ - extent_z + 1)
    rows = jnp.stack([column_x, lowest_y, lowest_y + extent_y, lowest_z, lowest_z + extent_z], -1)
    return rows.astype(jnp.int32)


def setup_inputs(seed: int = 0) -> dict:
    seeds = jax.random.split(jax.random.key(seed), 12)
    return {
        "velocity": draw_velocity(jax.random.fold_in(seeds[11], 71), 0),
        "eddy_viscosity": jnp.clip(jnp.exp(jax.random.uniform(seeds[1], (NZ,), jnp.float32, math.log(0.03), math.log(0.15))), 0.03, 0.15),
        "cell_height": draw_cell_height(jax.random.fold_in(seeds[11], 71), 0),
        "z_vectors": draw_z_vectors(jax.random.fold_in(seeds[11], 71), 0),
        "z_inverse": draw_z_inverse(jax.random.fold_in(seeds[11], 71), 0),
        "z_values": draw_z_values(jax.random.fold_in(seeds[11], 71), 0),
        "feed_source": draw_feed_source(jax.random.fold_in(seeds[11], 71), 0),
        "fringe_strength": jnp.clip(jnp.exp(jax.random.uniform(seeds[7], (DOMAINS,), jnp.float32, math.log(0.3), math.log(0.95))), 0.3, 0.95),
        "fringe_start": jax.random.randint(seeds[8], (1,), 0, NX - FRINGE + 1).astype(jnp.int32),
        "turbines": draw_turbines(jax.random.fold_in(seeds[11], 71), 0),
        "thrust": jnp.clip(jax.random.uniform(seeds[10], (DOMAINS, TURBINES), jnp.float32, 0.3, 0.9), 0.3, 0.9),
    }


HIGHEST = lax.Precision.HIGHEST

def cas_table(length):
    indices = jnp.arange(length, dtype=jnp.int32)
    residue = indices[:, None] * indices[None, :] % length
    angles = 2.0 * jnp.pi / length * residue.astype(jnp.float32)
    return jnp.cos(angles) + jnp.sin(angles)

def wave_term(indices, length):
    angles = 2.0 * jnp.pi / length * (indices % length).astype(jnp.float32)
    return 2.0 - 2.0 * jnp.cos(angles)

def hartley(values, cas_x, cas_y):
    along_x = jnp.einsum('kx,zxy->zky', cas_x, values, precision=HIGHEST)
    return jnp.einsum('zky,yl->zkl', along_x, cas_y, precision=HIGHEST)

def column_solve(columns, z_vectors, z_inverse, z_values, wave_x, wave_y):
    divisor_field = z_values[:, None, None] + wave_x[None, :, None] + wave_y[None, None, :]
    modal = jnp.einsum('kz,zxy->kxy', z_inverse, columns, precision=HIGHEST) / divisor_field
    return -jnp.einsum('zk,kxy->zxy', z_vectors, modal, precision=HIGHEST)

def diffuse(values, viscosity, heights):
    horizontal = jnp.roll(values, 1, 2) + jnp.roll(values, -1, 2) + jnp.roll(values, 1, 3) + jnp.roll(values, -1, 3) - 4.0 * values
    padded = jnp.pad(values, ((0, 0), (1, 1), (0, 0), (0, 0)))
    vertical = (padded[:, 2:] - 2.0 * values + padded[:, :-2]) / (heights * heights)[None, :, None, None]
    return values + viscosity[None, :, None, None] * (horizontal + vertical)

def reference(velocity, eddy_viscosity, cell_height, z_vectors, z_inverse, z_values, feed_source, fringe_strength, fringe_start, turbines, thrust):
    cas_x = cas_table(NX)
    cas_y = cas_table(NY)
    wave_x = wave_term(jnp.arange(NX, dtype=jnp.int32), NX)
    wave_y = wave_term(jnp.arange(NY, dtype=jnp.int32), NY)
    profile = jnp.sin(jnp.pi * (jnp.arange(FRINGE, dtype=jnp.float32) + 0.5) / FRINGE) ** 2
    fringe_begin = fringe_start[0]
    next_height = jnp.concatenate([cell_height[1:], jnp.zeros((1,), jnp.float32)])
    half_gap = 0.5 * (cell_height + next_height)
    span_x = jnp.arange(NX, dtype=jnp.int32)[None, :]
    span_y = jnp.arange(NY, dtype=jnp.int32)[None, :]
    levels = jnp.arange(NZ, dtype=jnp.int32)[None, :]
    windows = []
    for domain in range(DOMAINS):
        viscous_velocity = diffuse(velocity[domain].astype(jnp.float32), eddy_viscosity, cell_height)
        windows.append(lax.dynamic_slice_in_dim(viscous_velocity, fringe_begin, FRINGE, 2))
    forced_list = []
    results = []
    for domain in range(DOMAINS):
        viscous_velocity = diffuse(velocity[domain].astype(jnp.float32), eddy_viscosity, cell_height)
        window = windows[domain]
        candidates = jnp.stack(forced_list + windows[domain:])
        sources = feed_source[domain]
        target = jnp.stack([lax.dynamic_index_in_dim(candidates[:, component], sources[component], 0, keepdims=False) for component in range(3)])
        blend = fringe_strength[domain] * profile
        forced = window + blend[None, None, :, None] * (target - window)
        forced_list.append(forced)
        blended = lax.dynamic_update_slice_in_dim(viscous_velocity, forced, fringe_begin, 2)
        if domain == 0:
            flux_x = blended[0]
        else:
            table = turbines[domain]
            cells_x = (span_x == table[:, 0:1]).astype(jnp.float32)
            cells_y = ((span_y >= table[:, 1:2]) & (span_y < table[:, 2:3])).astype(jnp.float32)
            cells_z = ((levels >= table[:, 3:4]) & (levels < table[:, 4:5])).astype(jnp.float32)
            along = jnp.einsum('tx,zxy->tzy', cells_x, blended[0], precision=HIGHEST)
            sums = jnp.einsum('tzy,tz,ty->t', along, cells_z, cells_y, precision=HIGHEST)
            counts = ((table[:, 2] - table[:, 1]) * (table[:, 4] - table[:, 3])).astype(jnp.float32)
            disc_speed = sums / counts
            relay_updates = thrust[domain] * disc_speed * jnp.abs(disc_speed)
            spread = (relay_updates[:, None] * cells_z)[:, :, None] * cells_y[:, None, :]
            force = jnp.einsum('tx,tzy->zxy', cells_x, spread, precision=HIGHEST)
            flux_x = blended[0] - force
        flux_y = blended[1]
        flux_z = blended[2]
        divergence = flux_x - jnp.roll(flux_x, 1, 1) + (flux_y - jnp.roll(flux_y, 1, 2))
        shifted_down = jnp.concatenate([jnp.zeros_like(flux_z[:1]), flux_z[:-1]], 0)
        divergence = divergence + (flux_z - shifted_down) / cell_height[:, None, None]
        spectrum = hartley(divergence, cas_x, cas_y)
        solved = column_solve(spectrum, z_vectors, z_inverse, z_values, wave_x, wave_y)
        pressure = hartley(solved, cas_x, cas_y) / (NX * NY)
        shifted_up = jnp.concatenate([pressure[1:], jnp.zeros_like(pressure[:1])], 0)
        new_x = flux_x - (jnp.roll(pressure, -1, 1) - pressure)
        new_y = flux_y - (jnp.roll(pressure, -1, 2) - pressure)
        new_z = flux_z - (shifted_up - pressure) / half_gap[:, None, None]
        results.append(jnp.stack([new_x, new_y, new_z]).astype(jnp.bfloat16))
    return jnp.stack(results)
```

```python
import jax
import jax.numpy as jnp
import numpy as np
from jax import lax
from jax.experimental import pallas as pl
from jax.experimental.pallas import tpu as pltpu
from jax.sharding import Mesh, PartitionSpec as P

NX, NY, NZ = 512, 256, 128
FR = 32
ND = 8
NT = 8
BL = 16
KB = 64
HIGHEST = lax.Precision.HIGHEST
F32 = jnp.float32
BF16 = jnp.bfloat16
G = ("zb", "x", "c")
XC = ("x", "c")
VM = pl.BlockSpec(memory_space=pltpu.VMEM)
SM = pl.BlockSpec(memory_space=pltpu.SMEM)


def cas_numpy(length):
    j = np.arange(length, dtype=np.int64)
    angle = 2.0 * np.pi / length * ((j[:, None] * j[None, :]) % length)
    table = (np.cos(angle) + np.sin(angle)).astype(np.float32)
    hi = table.astype(jnp.bfloat16)
    lo = (table - hi.astype(np.float32)).astype(jnp.bfloat16)
    return np.stack([hi, lo])


def wave_term(indices, length):
    angles = 2.0 * jnp.pi / length * (indices % length).astype(F32)
    return 2.0 - 2.0 * jnp.cos(angles)


def cas_rows(rows, length):
    k = jnp.arange(length, dtype=jnp.int32)
    angles = 2.0 * jnp.pi / length * ((rows[:, None] * k[None, :]) % length).astype(F32)
    return jnp.cos(angles) + jnp.sin(angles)


def call(kernel, outs, *args, specs, scratch=(), name):
    return pl.pallas_call(
        kernel,
        out_shape=outs,
        in_specs=list(specs),
        out_specs=jax.tree.map(lambda _: VM, outs),
        scratch_shapes=list(scratch),
        name=name,
    )(*args)


def sds(shape, dtype=F32):
    return jax.ShapeDtypeStruct(shape, dtype)


def split(v):
    hi = v.astype(BF16)
    lo = (v - hi.astype(F32)).astype(BF16)
    return hi, lo


def dot3(a, b):
    ah, al = a
    bh, bl = b
    d = lambda p, q: jnp.dot(p, q, preferred_element_type=F32)
    return d(ah, bh) + (d(ah, bl) + d(al, bh))


def transform(value, cx_ref, cy_ref):
    along = dot3(split(value), (cy_ref[0], cy_ref[1]))
    return dot3((cx_ref[0], cx_ref[1]), split(along))


def forward_kernel(div_ref, cx_ref, cy_ref, out_ref):
    for z in range(2):
        out_ref[z] = transform(div_ref[z], cx_ref, cy_ref)


def inverse_kernel(level):
    def kernel(src_ref, cx_ref, cy_ref, out_ref):
        value = jnp.concatenate([src_ref[j, level * KB : (level + 1) * KB] for j in range(8)], 0)
        out_ref[...] = transform(value, cx_ref, cy_ref)

    return kernel


def weights_kernel(ids, feed, strength, profile_ref, out_ref, table, delta):
    y, zh = ids[0], ids[1]
    dom = y * 2 + zh
    lane = lax.broadcasted_iota(jnp.int32, (FR, 128), 1)

    def hot(e):
        slot = ((e // 2 - y) & 3) * 2 + ((e & 1) ^ zh)
        return (lane == slot).astype(F32)

    for d in range(ND):
        blend = strength[d] * profile_ref[...]
        own = hot(d)
        for c in range(3):
            s = feed[d * 3 + c]
            before = (s < d).astype(jnp.int32)
            earlier = table[jnp.minimum(s, d) * 3 + c]
            source = jnp.where(jnp.full((FR, 128), before) > 0, earlier, hot(s))
            change = blend * (source - own)
            delta[d * 3 + c] = change
            table[d * 3 + c] = own + change
    row = lax.broadcasted_iota(jnp.int32, (FR, 128), 0)
    for c in range(3):
        w = delta[dom * 3 + c]
        out_ref[0, c] = w
        out_ref[1, c] = jnp.where(row == 0, 0.0, pltpu.roll(w, 1, 0))
        out_ref[2, c] = jnp.where(row == FR - 1, 0.0, pltpu.roll(w, FR - 1, 0))


def combine_kernel(nu, ih2, w_ref, *refs):
    raws = refs[:ND]
    loc_ref, up_ref, dn_ref = refs[ND:]
    row = lax.broadcasted_iota(jnp.int32, (FR, NY), 0)
    for c in range(3):
        acc, lap = [], []
        for z in range(2):
            p = c * 2 + z
            a0 = jnp.zeros((FR, NY), F32)
            am = jnp.zeros((FR, NY), F32)
            ap = jnp.zeros((FR, NY), F32)
            e0 = jnp.zeros((1, NY), F32)
            e1 = jnp.zeros((1, NY), F32)
            for e in range(ND):
                v = raws[e][p * FR : (p + 1) * FR].astype(F32)
                edge = raws[e][6 * FR : 6 * FR + 16].astype(F32)
                a0 = a0 + w_ref[0, c, :, e : e + 1] * v
                am = am + w_ref[1, c, :, e : e + 1] * v
                ap = ap + w_ref[2, c, :, e : e + 1] * v
                e0 = e0 + w_ref[0, c, 0:1, e : e + 1] * edge[p : p + 1]
                e1 = e1 + w_ref[0, c, FR - 1 : FR, e : e + 1] * edge[6 + p : 7 + p]
            xs = pltpu.roll(am, FR - 1, 0) + pltpu.roll(ap, 1, 0)
            xs = xs + jnp.where(row == 0, e0, 0.0) + jnp.where(row == FR - 1, e1, 0.0)
            ys = pltpu.roll(a0, 1, 1) + pltpu.roll(a0, NY - 1, 1)
            acc.append(a0)
            lap.append(xs + ys - 4.0 * a0)
        for z in range(2):
            loc_ref[c * 2 + z] = acc[z] + nu[z] * (lap[z] + (acc[1 - z] - 2.0 * acc[z]) * ih2[z])
        up_ref[c] = acc[1]
        dn_ref[c] = acc[0]
        if c == 2:
            up_ref[3] = acc[0]
            up_ref[4] = lap[1]


def delta_kernel(nu, ih2, tab, x0_ref, off_ref, loc_ref, vup_ref, vdn_ref, dn_ref, stream_ref, d_ref, dd_ref, part_ref):
    for c in range(3):
        d_ref[c * 2] = loc_ref[c * 2] + (nu[0] * ih2[0]) * vup_ref[c]
        d_ref[c * 2 + 1] = loc_ref[c * 2 + 1] + (nu[1] * ih2[1]) * vdn_ref[c]
    under = vup_ref[2] + nu[2] * (vup_ref[4] + (dn_ref[2] - 2.0 * vup_ref[2] + vup_ref[3]) * ih2[2])
    zero = jnp.zeros((8, NY), F32)
    ext = lambda v: jnp.concatenate([v, zero], 0)
    for z in range(2):
        du = ext(d_ref[z])
        dv = d_ref[2 + z]
        below = under if z == 0 else d_ref[4]
        rest = dv - pltpu.roll(dv, 1, 1) + (d_ref[4 + z] - below) * ih2[3 + z]
        dd_ref[z] = du - pltpu.roll(du, 1, 0) + ext(rest)
    lane = lax.broadcasted_iota(jnp.int32, (1, NY), 1)
    x0 = x0_ref[0]
    off = off_ref[0]
    for t in range(NT):
        col = tab[t, 0]
        inside = jnp.logical_and(col >= x0, col < x0 + FR)
        i = jnp.where(inside, col - x0, 0)
        flag = jnp.where(inside, 1.0, 0.0)
        total = jnp.zeros((1, NY), F32)
        for z in range(2):
            line = stream_ref[z, pl.ds(col, 1), :] + flag * d_ref[z, pl.ds(i, 1), :]
            lev = off + z
            keep = jnp.where(jnp.logical_and(lev >= tab[t, 3], lev < tab[t, 4]), 1.0, 0.0)
            total = total + keep * line
        span = jnp.logical_and(lane >= tab[t, 1], lane < tab[t, 2])
        part_ref[t : t + 1] = jnp.where(span, total, 0.0)


def correct_kernel(main_ref, dd_ref, rows_ref, cy_ref, out_ref):
    cy = cy_ref[0].astype(F32) + cy_ref[1].astype(F32)
    for z in range(2):
        along = jnp.dot(dd_ref[z], cy, preferred_element_type=F32, precision=HIGHEST)
        extra = lax.dot_general(
            rows_ref[...], along, (((0,), (0,)), ((), ())), precision=HIGHEST, preferred_element_type=F32
        )
        for j in range(8):
            out_ref[j, z * KB : (z + 1) * KB] = (
                main_ref[z, j * KB : (j + 1) * KB] + extra[j * KB : (j + 1) * KB]
            )


def factor_kernel(h, c, cm, ids, lam_ref, r_ref, q_ref, d_ref, up_ref, dn_ref, pu, pd, au, ad, al):
    b = ids[0]
    lam = lam_ref[...]
    one = jnp.ones((KB, NY), F32)

    def up_block(bb, alpha):
        au[bb] = alpha

        def step(i, carry):
            n, d, pr = carry
            z = bb * BL + i
            e = n + cm[z] * d
            return (lam * h[z]) * e + n * cm[z], e, pr * cm[z]

        n, d, pr = lax.fori_loop(0, BL, step, (alpha, one, F32(1.0)), unroll=4)
        inv = 1.0 / d
        pu[bb] = pr * inv
        return n * inv

    lax.fori_loop(0, 8, up_block, one)

    def dn_block(j, beta):
        bb = 7 - j
        ad[bb] = beta
        first = jnp.where(j == 0, 0.0, 1.0)

        def step(i, carry):
            n, d, pr = carry
            z = bb * BL + BL - 1 - i
            e = n + c[z] * d
            return (lam * h[z]) * e + n * c[z], e, pr * c[z]

        n, d, pr = lax.fori_loop(0, BL, step, (beta, one * first, first), unroll=4)
        inv = 1.0 / d
        pd[bb] = pr * inv
        return n * inv

    lax.fori_loop(0, 8, dn_block, one)

    def own_up(i, alpha):
        z = b * BL + i
        r = cm[z] / (alpha + cm[z])
        alpha = lam * h[z] + alpha * r
        r_ref[i] = r
        al[i] = alpha
        return alpha

    lax.fori_loop(0, BL, own_up, au[b])

    def own_dn(j, beta):
        i = BL - 1 - j
        z = b * BL + i
        keep = jnp.where(jnp.logical_and(b == 7, j == 0), 0.0, 1.0)
        inv = c[z] / (beta + c[z] * keep)
        through = beta * inv
        q_ref[i] = inv * keep
        d_ref[i] = (1.0 / (NX * NY)) / (al[i] + through)
        return lam * h[z] + through

    lax.fori_loop(0, BL, own_dn, ad[b])
    low = lambda k: jnp.maximum(b - k, 0)
    top = lambda k: jnp.minimum(b + k, 7)
    p1 = pu[low(1)]
    p2 = p1 * pu[low(2)]
    up_ref[0] = p1
    up_ref[1] = p2
    up_ref[2] = p2 * pu[low(3)] * pu[low(4)]
    q1 = pd[top(1)]
    q2 = q1 * pd[top(2)]
    dn_ref[0] = q1
    dn_ref[1] = q2
    dn_ref[2] = q2 * pd[top(3)] * pd[top(4)]


def sweep_kernel(h, ids, zlo, zhi, thr_ref, col_ref, o_ref, r_ref, q_ref, rhs_ref, s_ref, t_ref, f_ref):
    b = ids[0]
    sums = col_ref[0, 2 * KB :]
    for j in range(1, 8):
        sums = sums + col_ref[j, 2 * KB :]
    total = jnp.sum(sums, axis=1, keepdims=True)
    speed = total * thr_ref[:, 1:2]
    force = thr_ref[:, 0:1] * speed * jnp.abs(speed)
    f_ref[...] = jnp.broadcast_to(force, (NT, 128))
    carry = jnp.zeros((KB, NY), F32)
    for i in range(BL):
        z = b * BL + i
        rhs_ref[i] = col_ref[i // 2, (i % 2) * KB : (i % 2 + 1) * KB]
    for t in range(NT):
        for i in range(BL):
            z = b * BL + i

            @pl.when(jnp.logical_and(z >= zlo[t], z < zhi[t]))
            def _():
                rhs_ref[i] = rhs_ref[i] + force[t : t + 1] * o_ref[t]

    for i in range(BL):
        v = rhs_ref[i] * (-h[b * BL + i])
        rhs_ref[i] = v
        carry = v + r_ref[i] * carry
    s_ref[...] = carry
    carry = jnp.zeros((KB, NY), F32)
    for i in reversed(range(BL)):
        carry = rhs_ref[i] + q_ref[i] * carry
    t_ref[...] = carry


def solve_kernel(rhs_ref, r_ref, q_ref, d_ref, i_ref, j_ref, out_ref):
    f = i_ref[...]
    for i in range(BL):
        f = rhs_ref[i] + r_ref[i] * f
        out_ref[i] = f
    g = j_ref[...]
    for i in reversed(range(BL)):
        g = rhs_ref[i] + q_ref[i] * g
        out_ref[i] = (out_ref[i] + (g - rhs_ref[i])) * d_ref[i]


def body(
    velocity, eddy_viscosity, cell_height, z_vectors, z_inverse, z_values,
    feed_source, fringe_strength, fringe_start, turbines, thrust,
):
    u = velocity[0]
    yi, zhi_, zb = lax.axis_index("y"), lax.axis_index("zh"), lax.axis_index("zb")
    lane_id = lax.axis_index(XC)
    slab = lax.axis_index(G)
    dom = yi * 2 + zhi_
    off = slab * 2
    up_perm = [(k, k + 1) for k in range(63)]
    dn_perm = [(k + 1, k) for k in range(63)]
    x0 = fringe_start[0]

    main = lax.dynamic_slice(u, (0, 0, x0, 0), (3, 2, FR, NY)).reshape(6 * FR, NY)
    left = lax.dynamic_slice(u, (0, 0, (x0 + NX - 1) % NX, 0), (3, 2, 1, NY)).reshape(6, NY)
    right = lax.dynamic_slice(u, (0, 0, (x0 + FR) % NX, 0), (3, 2, 1, NY)).reshape(6, NY)
    raw = jnp.concatenate([main, left, right, jnp.zeros((4, NY), BF16)], 0)
    other = lax.ppermute(raw, "zh", [(0, 1), (1, 0)])
    around = lambda v, s: lax.ppermute(v, "y", [(k, (k + s) % 4) for k in range(4)])
    below = lax.ppermute(jnp.concatenate([u[:, 1], u[2:3, 0]], 0), G, up_perm)
    above = lax.ppermute(u[:, 0], G, dn_perm)
    raws = [raw, other]
    own_ring = [around(raw, 3), around(raw, 2), around(raw, 1)]
    other_ring = [around(other, 3), around(other, 2), around(other, 1)]
    for a, o in zip(own_ring, other_ring):
        raws += [a, o]

    next_height = jnp.concatenate([cell_height[1:], jnp.zeros((1,), F32)])
    half_gap = 0.5 * (cell_height + next_height)
    coupling = 1.0 / half_gap
    coupling_below = jnp.concatenate([jnp.zeros((1,), F32), coupling[:-1]])
    heights = lax.dynamic_slice_in_dim(cell_height, off, 2, 0)
    viscous = lax.dynamic_slice_in_dim(eddy_viscosity, off, 2, 0)
    local_gap = lax.dynamic_slice_in_dim(half_gap, off, 2, 0)
    low = jnp.maximum(off - 1, 0)
    has_low = (off > 0).astype(F32)
    nu_low = eddy_viscosity[low] * has_low
    h_low = cell_height[low]
    nu = jnp.concatenate([viscous, nu_low[None]])
    ih2 = jnp.concatenate([1.0 / (heights * heights), (1.0 / (h_low * h_low))[None], 1.0 / heights])
    table = lax.dynamic_index_in_dim(turbines, dom, 0, keepdims=False)
    active = (dom > 0).astype(F32)
    own_thrust = lax.dynamic_index_in_dim(thrust, dom, 0, keepdims=False) * active
    counts = ((table[:, 2] - table[:, 1]) * (table[:, 4] - table[:, 3])).astype(F32)
    thr = jnp.stack([own_thrust, 1.0 / counts], 1)
    ids = jnp.stack([yi, zhi_]).astype(jnp.int32)
    bid = zb[None].astype(jnp.int32)

    cx = jnp.asarray(cas_numpy(NX))
    cy = jnp.asarray(cas_numpy(NY))

    k_own = lane_id * KB + jnp.arange(KB, dtype=jnp.int32)
    lam = wave_term(k_own, NX)[:, None] + wave_term(jnp.arange(NY, dtype=jnp.int32), NY)[None, :]
    plane = (KB, NY)
    r, q, inv_den, pu, pd = call(
        factor_kernel,
        (sds((BL, *plane)), sds((BL, *plane)), sds((BL, *plane)), sds((3, *plane)), sds((3, *plane))),
        cell_height, coupling, coupling_below, bid, lam,
        specs=[SM, SM, SM, SM, VM],
        scratch=[pltpu.VMEM((8, *plane), F32)] * 4 + [pltpu.VMEM((BL, *plane), F32)],
        name="factors",
    )
    profile = jnp.sin(jnp.pi * (jnp.arange(FR, dtype=F32) + 0.5) / FR) ** 2
    weights = call(
        weights_kernel, sds((3, 3, FR, 128)),
        ids, feed_source.reshape(-1), fringe_strength, jnp.broadcast_to(profile[:, None], (FR, 128)),
        specs=[SM, SM, SM, VM],
        scratch=[pltpu.VMEM((24, FR, 128), F32)] * 2,
        name="weights",
    )
    rows = cas_rows((x0 + jnp.arange(40, dtype=jnp.int32)) % NX, NX)
    k_f = k_own[None, :]
    ang = lambda col: 2.0 * jnp.pi / NX * ((col[:, None] * k_f) % NX).astype(F32)
    cas = lambda a: jnp.cos(a) + jnp.sin(a)
    ax = cas(ang(table[:, 0] + 1)) - cas(ang(table[:, 0]))
    span_y = jnp.arange(NY, dtype=jnp.int32)[None, :]
    cells_y = ((span_y >= table[:, 1:2]) & (span_y < table[:, 2:3])).astype(F32)
    cy32 = cy[0].astype(F32) + cy[1].astype(F32)
    by = jnp.dot(cells_y, cy32, precision=HIGHEST)
    outer = ax[:, :, None] * by[:, None, :]

    center = u.astype(F32)
    lo = below.astype(F32)
    hi = above.astype(F32)
    horizontal = lambda v: (
        jnp.roll(v, 1, -2) + jnp.roll(v, -1, -2) + jnp.roll(v, 1, -1) + jnp.roll(v, -1, -1) - 4.0 * v
    )
    stack = jnp.concatenate([lo[:3, None], center, hi[:, None]], 1)
    vertical = (stack[:, 2:] - 2.0 * center + stack[:, :-2]) * ih2[:2][None, :, None, None]
    diff = center + viscous[None, :, None, None] * (horizontal(center) + vertical)
    w_low = lo[2] + nu_low * (horizontal(lo[2]) + (center[2, 0] - 2.0 * lo[2] + lo[3]) * ih2[2])
    shifted = jnp.stack([w_low, diff[2, 0]])
    div = (
        diff[0] - jnp.roll(diff[0], 1, 1)
        + (diff[1] - jnp.roll(diff[1], 1, 2))
        + (diff[2] - shifted) * ih2[3:][:, None, None]
    )
    spec_main = call(forward_kernel, sds((2, NX, NY)), div, cx, cy, specs=[VM] * 3, name="forward")

    loc, vup_s, vdn_s = call(
        combine_kernel, (sds((6, FR, NY)), sds((5, FR, NY)), sds((3, FR, NY))),
        nu, ih2, weights, *raws,
        specs=[SM, SM] + [VM] * 9,
        name="combine",
    )
    vup = lax.ppermute(vup_s, G, up_perm)
    vdn = lax.ppermute(vdn_s, G, dn_perm)
    delta, ddiv, part = call(
        delta_kernel, (sds((6, FR, NY)), sds((2, 40, NY)), sds((NT, NY))),
        nu, ih2, table, x0[None], off[None].astype(jnp.int32), loc, vup, vdn, vdn_s, diff[0],
        specs=[SM] * 5 + [VM] * 5,
        name="delta",
    )
    p_up = lax.ppermute(part, "zb", [(k, k + 1) for k in range(7)])
    p_dn = lax.ppermute(part, "zb", [(k + 1, k) for k in range(7)])
    spectrum = call(
        correct_kernel, sds((8, 2 * KB, NY)), spec_main, ddiv, rows, cy, specs=[VM] * 4, name="correct"
    )
    sums = jnp.broadcast_to((part + p_up + p_dn)[None], (8, NT, NY))
    columns = lax.all_to_all(jnp.concatenate([spectrum, sums], 1), XC, 0, 0, tiled=True)

    rhs, s, t, force = call(
        sweep_kernel, (sds((BL, *plane)), sds(plane), sds(plane), sds((NT, 128))),
        cell_height, bid, table[:, 3], table[:, 4], thr, columns, outer, r, q,
        specs=[SM] * 4 + [VM] * 5,
        name="sweep",
    )
    climb = lambda v, k: lax.ppermute(v, "zb", [(j, j + k) for j in range(8 - k)])
    drop = lambda v, k: lax.ppermute(v, "zb", [(j + k, j) for j in range(8 - k)])
    a = climb(s, 1) + pu[0] * climb(s, 2)
    e = drop(t, 1) + pd[0] * drop(t, 2)
    a, e = a + pu[1] * climb(a, 2), e + pd[1] * drop(e, 2)
    a, e = a + pu[2] * climb(a, 4), e + pd[2] * drop(e, 4)
    solved = call(
        solve_kernel, sds((BL, *plane)), rhs, r, q, inv_den, a, e, specs=[VM] * 6, name="solve"
    )
    returned = lax.all_to_all(solved.reshape(8, 2 * KB, NY), XC, 0, 0, tiled=True)

    window = lax.dynamic_slice(diff, (0, 0, x0, 0), (3, 2, FR, NY)) + delta.reshape(3, 2, FR, NY)
    blended = lax.dynamic_update_slice(diff, window, (0, 0, x0, 0))
    cells_x = (jnp.arange(NX, dtype=jnp.int32)[None, :] == table[:, 0:1]).astype(F32)
    levels = off + jnp.arange(2, dtype=jnp.int32)[None, :]
    cells_z = ((levels >= table[:, 3:4]) & (levels < table[:, 4:5])).astype(F32)
    spread = (force[:, 0:1] * cells_z)[:, :, None] * cells_y[:, None, :]
    flux_x = blended[0] - jnp.einsum("tx,tzy->zxy", cells_x, spread, precision=HIGHEST)

    p0 = call(inverse_kernel(0), sds((NX, NY)), returned, cx, cy, specs=[VM] * 3, name="inverse0")
    p2 = lax.ppermute(p0, G, dn_perm)
    p1 = call(inverse_kernel(1), sds((NX, NY)), returned, cx, cy, specs=[VM] * 3, name="inverse1")
    pressure = jnp.stack([p0, p1])
    shifted_up = jnp.stack([p1, p2])
    new_x = flux_x - (jnp.roll(pressure, -1, 1) - pressure)
    new_y = blended[1] - (jnp.roll(pressure, -1, 2) - pressure)
    new_z = blended[2] - (shifted_up - pressure) / local_gap[:, None, None]
    return jnp.stack([new_x, new_y, new_z])[None].astype(BF16)


def solution(mesh):
    fine = Mesh(mesh.devices.reshape(4, 2, 8, 4, 2), ("y", "zh", "zb", "x", "c"))
    spec = P(("y", "zh"), None, ("zb", "x", "c"), None, None)
    return jax.shard_map(
        body, mesh=fine, in_specs=(spec,) + (P(),) * 10, out_specs=spec, check_vma=False
    )
```

```python
import jax
import jax.numpy as jnp
import numpy as np
from jax import lax
from jax.experimental import pallas as pl
from jax.experimental.pallas import tpu as pltpu
from jax.sharding import Mesh, PartitionSpec as P

NX, NY, NZ = 512, 256, 128
FR = 32
ND = 8
NT = 8
RAW = 208
BL = 16
KB = 64
HIGHEST = lax.Precision.HIGHEST
F32 = jnp.float32
BF16 = jnp.bfloat16
G = ("zb", "x", "c")
XC = ("x", "c")
VM = pl.BlockSpec(memory_space=pltpu.VMEM)
SM = pl.BlockSpec(memory_space=pltpu.SMEM)


def split_numpy(table):
    table = table.astype(np.float32)
    hi = table.astype(jnp.bfloat16)
    lo = (table - hi.astype(np.float32)).astype(jnp.bfloat16)
    return np.stack([hi, lo])


def cas_numpy(rows, cols, length):
    angle = 2.0 * np.pi / length * ((rows[:, None] * cols[None, :]) % length)
    return np.cos(angle) + np.sin(angle)


HALF = np.arange(NX // 2, dtype=np.int64)
CAS = split_numpy(cas_numpy(HALF, HALF, NY))
ODD = split_numpy(cas_numpy(2 * HALF + 1, HALF, NX))
ODD_T = split_numpy(cas_numpy(HALF, 2 * HALF + 1, NX))
PROFILE = np.broadcast_to(np.sin(np.pi * (np.arange(FR) + 0.5) / FR)[:, None] ** 2, (FR, 128)).astype(np.float32)
CH = 64


def wave_term(indices, length):
    angles = 2.0 * jnp.pi / length * (indices % length).astype(F32)
    return 2.0 - 2.0 * jnp.cos(angles)


def call(kernel, outs, *args, specs, scratch=(), name):
    return pl.pallas_call(
        kernel,
        out_shape=outs,
        in_specs=list(specs),
        out_specs=jax.tree.map(lambda _: VM, outs),
        scratch_shapes=list(scratch),
        name=name,
    )(*args)


def sds(shape, dtype=F32):
    return jax.ShapeDtypeStruct(shape, dtype)


def split(v):
    hi = v.astype(BF16)
    lo = (v - hi.astype(F32)).astype(BF16)
    return hi, lo


def dot3(a, b):
    ah, al = a
    bh, bl = b
    d = lambda p, q: jnp.dot(p, q, preferred_element_type=F32)
    return d(ah, bh) + (d(ah, bl) + d(al, bh))


def pair(ref):
    return ref[0], ref[1]


def inverse_transform(src_ref, level, cas_ref, oddt_ref):
    value = jnp.concatenate([src_ref[j, level * KB : (level + 1) * KB] for j in range(8)], 0)
    along = dot3(split(value), pair(cas_ref))
    even = dot3(pair(cas_ref), split(along[: NX // 2]))
    odd = dot3(pair(oddt_ref), split(along[NX // 2 :]))
    return even + odd, even - odd


def rows_of(shape):
    return lax.broadcasted_iota(jnp.int32, shape, 0)


def main_kernel(
    heights, visc, ids, tab, u_ref, lo_ref, hi_ref, cas_ref, odd_ref, diff_ref, spec_ref, line_ref, x, dv, wl
):
    off, dom = ids[6], ids[5]
    row = rows_of((CH, NY))
    low = jnp.maximum(off - 1, 0)
    nu = [visc[off], visc[off + 1], jnp.where(off > 0, visc[low], 0.0)]
    full = lambda v: jnp.full((1, NY), v, F32)
    hs = [full(heights[off]), full(heights[off + 1]), full(heights[low])]
    ih = [1.0 / v for v in hs]
    ih2 = [1.0 / (v * v) for v in hs]

    def load(i, _):
        r = pl.ds(pl.multiple_of(i * CH, CH), CH)
        for c in range(3):
            x[c * 4, r] = lo_ref[c, r].astype(F32)
            x[c * 4 + 1, r] = u_ref[c, 0, r].astype(F32)
            x[c * 4 + 2, r] = u_ref[c, 1, r].astype(F32)
            x[c * 4 + 3, r] = hi_ref[c, r].astype(F32)
        x[12, r] = lo_ref[3, r].astype(F32)
        return 0

    lax.fori_loop(0, NX // CH, load, 0)

    def diffuse(i, _):
        r0 = pl.multiple_of(i * CH, CH)
        r = pl.ds(r0, CH)
        before = jnp.where(r0 == 0, NX - 1, r0 - 1)
        after = (r0 + CH) & (NX - 1)

        def apply(p, down, up, k):
            v = x[p, r]
            xs = jnp.where(row == 0, x[p, pl.ds(before, 1)], pltpu.roll(v, 1, 0)) + jnp.where(
                row == CH - 1, x[p, pl.ds(after, 1)], pltpu.roll(v, CH - 1, 0)
            )
            ys = pltpu.roll(v, 1, 1) + pltpu.roll(v, NY - 1, 1)
            return v + nu[k] * ((xs + ys - 4.0 * v) + (x[up, r] - 2.0 * v + x[down, r]) * ih2[k])

        for c in range(3):
            diff_ref[c, 0, r] = apply(c * 4 + 1, c * 4, c * 4 + 2, 0)
            diff_ref[c, 1, r] = apply(c * 4 + 2, c * 4 + 1, c * 4 + 3, 1)
        wl[r] = apply(8, 12, 9, 2)
        return 0

    lax.fori_loop(0, NX // CH, diffuse, 0)

    def diverge(i, _):
        r0 = pl.multiple_of(i * CH, CH)
        r = pl.ds(r0, CH)
        before = jnp.where(r0 == 0, NX - 1, r0 - 1)
        for z in range(2):
            a = diff_ref[0, z, r]
            b = diff_ref[1, z, r]
            under = wl[r] if z == 0 else diff_ref[2, 0, r]
            back = jnp.where(row == 0, diff_ref[0, z, pl.ds(before, 1)], pltpu.roll(a, 1, 0))
            dv[z, r] = (a - back) + (b - pltpu.roll(b, 1, 1)) + (diff_ref[2, z, r] - under) * ih[z]
        return 0

    lax.fori_loop(0, NX // CH, diverge, 0)
    for t in range(NT):
        for z in range(2):
            line_ref[z, t : t + 1] = diff_ref[0, z, pl.ds(tab[dom, t, 0], 1)]
    half = NX // 2
    for z in range(2):
        along = dot3(split(dv[z]), pair(cas_ref))
        spec_ref[z, :half] = dot3(pair(cas_ref), split(along[:half] + along[half:]))
        spec_ref[z, half:] = dot3(pair(odd_ref), split(along[:half] - along[half:]))


def first_kernel(src_ref, cas_ref, oddt_ref, out_ref):
    a, b = inverse_transform(src_ref, 0, cas_ref, oddt_ref)
    out_ref[: NX // 2] = a
    out_ref[NX // 2 :] = b


def final_kernel(heights, ids, src_ref, p0_ref, flow_ref, cas_ref, oddt_ref, out_ref, p1_ref):
    off = ids[6]
    a, b = inverse_transform(src_ref, 1, cas_ref, oddt_ref)
    p1_ref[: NX // 2] = a
    p1_ref[NX // 2 :] = b
    row = rows_of((CH, NY))
    gap = 2.0 / jnp.full((1, NY), heights[off] + heights[off + 1], F32)

    def step(i, _):
        r0 = pl.multiple_of(i * CH, CH)
        r = pl.ds(r0, CH)
        after = (r0 + CH) & (NX - 1)
        for z, ref in ((0, p0_ref), (1, p1_ref)):
            p = ref[r]
            ahead = jnp.where(row == CH - 1, ref[pl.ds(after, 1)], pltpu.roll(p, CH - 1, 0))
            out_ref[0, 0, z, r] = (flow_ref[0, z, r] - (ahead - p)).astype(BF16)
            out_ref[0, 1, z, r] = (flow_ref[1, z, r] - (pltpu.roll(p, NY - 1, 1) - p)).astype(BF16)
        out_ref[0, 2, 0, r] = (flow_ref[2, 0, r] - (p1_ref[r] - p0_ref[r]) * gap).astype(BF16)
        return 0

    lax.fori_loop(0, NX // CH, step, 0)


def top_kernel(heights, ids, _, p1_ref, p2_ref, flow_ref, out_ref):
    off = ids[6]
    above = jnp.where(off + 2 < NZ, heights[jnp.minimum(off + 2, NZ - 1)], 0.0)
    gap = 2.0 / jnp.full((1, NY), heights[off + 1] + above, F32)

    def step(i, _):
        r = pl.ds(pl.multiple_of(i * CH, CH), CH)
        out_ref[0, 0, 0, r] = (flow_ref[0, 0, r] - (p2_ref[r] - p1_ref[r]) * gap).astype(BF16)
        return 0

    lax.fori_loop(0, NX // CH, step, 0)


def blend_kernel(ids, x0s, tab, delta_ref, force_ref, diff_ref, out_ref):
    off, dom, x0 = ids[6], ids[5], x0s[0]
    out_ref[...] = diff_ref[...]

    def step(i, _):
        for c in range(3):
            for z in range(2):
                r = pl.ds(x0 + i, 1)
                out_ref[c, z, r] = out_ref[c, z, r] + delta_ref[c * 2 + z, pl.ds(i, 1)]
        return 0

    lax.fori_loop(0, FR, step, 0)
    lane = lax.broadcasted_iota(jnp.int32, (1, NY), 1)
    for t in range(NT):
        span = jnp.logical_and(lane >= tab[dom, t, 1], lane < tab[dom, t, 2])
        line = jnp.where(span, jnp.broadcast_to(force_ref[t : t + 1, 0:1], (1, NY)), 0.0)
        for z in range(2):
            lev = off + z
            keep = jnp.where(jnp.logical_and(lev >= tab[dom, t, 3], lev < tab[dom, t, 4]), 1.0, 0.0)
            r = pl.ds(tab[dom, t, 0], 1)
            out_ref[0, z, r] = out_ref[0, z, r] - keep * line


def weights_kernel(ids, feed, strength, profile_ref, out_ref, table, delta):
    y, zh = ids[0], ids[1]
    dom = y * 2 + zh
    lane = lax.broadcasted_iota(jnp.int32, (FR, 128), 1)

    def hot(e):
        slot = ((e // 2 - y) & 3) * 2 + ((e & 1) ^ zh)
        return (lane == slot).astype(F32)

    for d in range(ND):
        blend = strength[d] * profile_ref[...]
        own = hot(d)
        for c in range(3):
            s = feed[d, c]
            before = (s < d).astype(jnp.int32)
            earlier = table[jnp.minimum(s, d) * 3 + c]
            source = jnp.where(jnp.full((FR, 128), before) > 0, earlier, hot(s))
            change = blend * (source - own)
            delta[d * 3 + c] = change
            table[d * 3 + c] = own + change
    row = lax.broadcasted_iota(jnp.int32, (FR, 128), 0)
    for c in range(3):
        w = delta[dom * 3 + c]
        out_ref[0, c] = w
        out_ref[1, c] = jnp.where(row == 0, 0.0, pltpu.roll(w, 1, 0))
        out_ref[2, c] = jnp.where(row == FR - 1, 0.0, pltpu.roll(w, FR - 1, 0))


def level_terms(heights, visc, off):
    low = jnp.maximum(off - 1, 0)
    nu = [visc[off], visc[off + 1], jnp.where(off > 0, visc[low], 0.0)]
    full = lambda v: jnp.full((1, NY), v, F32)
    hs = [full(heights[off]), full(heights[off + 1]), full(heights[low])]
    return nu, [1.0 / v for v in hs], [1.0 / (v * v) for v in hs]


def combine_kernel(heights, visc, ids, tab, x0s, w_ref, line_ref, *refs):
    off, dom, x0 = ids[6], ids[5], x0s[0]
    nu, _, ih2 = level_terms(heights, visc, off)
    slots = refs[:ND]
    loc_ref, up_ref, dn_ref, part_ref = refs[ND:]
    row = rows_of((FR, NY))
    for c in range(3):
        acc, lap = [], []
        for z in range(2):
            p = c * 2 + z
            a0 = jnp.zeros((FR, NY), F32)
            am = jnp.zeros((FR, NY), F32)
            ap = jnp.zeros((FR, NY), F32)
            e0 = jnp.zeros((1, NY), F32)
            e1 = jnp.zeros((1, NY), F32)
            for e, ref in enumerate(slots):
                v = ref[p * FR : (p + 1) * FR].astype(F32)
                edge = ref[6 * FR : RAW].astype(F32)
                a0 = a0 + w_ref[0, c, :, e : e + 1] * v
                am = am + w_ref[1, c, :, e : e + 1] * v
                ap = ap + w_ref[2, c, :, e : e + 1] * v
                e0 = e0 + w_ref[0, c, 0:1, e : e + 1] * edge[p : p + 1]
                e1 = e1 + w_ref[0, c, FR - 1 : FR, e : e + 1] * edge[6 + p : 7 + p]
            xs = pltpu.roll(am, FR - 1, 0) + pltpu.roll(ap, 1, 0)
            xs = xs + jnp.where(row == 0, e0, 0.0) + jnp.where(row == FR - 1, e1, 0.0)
            ys = pltpu.roll(a0, 1, 1) + pltpu.roll(a0, NY - 1, 1)
            acc.append(a0)
            lap.append(xs + ys - 4.0 * a0)
        for z in range(2):
            loc_ref[c * 2 + z] = acc[z] + nu[z] * (lap[z] + (acc[1 - z] - 2.0 * acc[z]) * ih2[z])
        up_ref[c] = acc[1]
        dn_ref[c] = acc[0]
        if c == 2:
            up_ref[3] = acc[0]
            up_ref[4] = lap[1]


    high = jnp.minimum(off + 2, NZ - 1)
    spill = (ih2[2] * nu[2], visc[high] / jnp.full((1, NY), heights[high] * heights[high], F32))
    lane = lax.broadcasted_iota(jnp.int32, (1, NY), 1)
    for t in range(NT):
        col = tab[dom, t, 0]
        inside = jnp.logical_and(col >= x0, col < x0 + FR)
        i = pl.ds(jnp.where(inside, col - x0, 0), 1)
        flag = jnp.where(inside, 1.0, 0.0)

        def keep(lev):
            return jnp.where(jnp.logical_and(lev >= tab[dom, t, 3], lev < tab[dom, t, 4]), 1.0, 0.0)

        total = keep(off) * line_ref[0, t : t + 1] + keep(off + 1) * line_ref[1, t : t + 1]
        total = total + (flag * keep(off)) * loc_ref[0, i] + (flag * keep(off + 1)) * loc_ref[1, i]
        total = total + (flag * keep(off - 1)) * (spill[0] * dn_ref[0, i])
        total = total + (flag * keep(off + 2)) * (spill[1] * up_ref[0, i])
        span = jnp.logical_and(lane >= tab[dom, t, 1], lane < tab[dom, t, 2])
        part_ref[t : t + 1] = jnp.where(span, total, 0.0)


def correct_kernel(
    heights, visc, ids, loc_ref, vup_ref, vdn_ref, dn_ref, part_ref, pup_ref, pdn_ref, main_ref, rows_ref, cas_ref,
    out_ref, d_ref,
):
    nu, ih, ih2 = level_terms(heights, visc, ids[6])
    for c in range(3):
        d_ref[c * 2] = loc_ref[c * 2] + (nu[0] * ih2[0]) * vup_ref[c]
        d_ref[c * 2 + 1] = loc_ref[c * 2 + 1] + (nu[1] * ih2[1]) * vdn_ref[c]
    under = vup_ref[2] + nu[2] * (vup_ref[4] + (dn_ref[2] - 2.0 * vup_ref[2] + vup_ref[3]) * ih2[2])
    zero = jnp.zeros((8, NY), F32)
    ext = lambda v: jnp.concatenate([v, zero], 0)
    rows = split(rows_ref[...])
    sums = part_ref[...] + pup_ref[...] + pdn_ref[...]
    for z in range(2):
        du = ext(d_ref[z])
        dv = d_ref[2 + z]
        below = under if z == 0 else d_ref[4]
        rest = dv - pltpu.roll(dv, 1, 1) + (d_ref[4 + z] - below) * ih[z]
        change = du - pltpu.roll(du, 1, 0) + ext(rest)
        along = dot3(split(change), pair(cas_ref))
        extra = dot3(rows, split(along))
        for j in range(8):
            out_ref[j, z * KB : (z + 1) * KB] = (
                main_ref[z, j * KB : (j + 1) * KB] + extra[j * KB : (j + 1) * KB]
            )
            out_ref[j, 2 * KB :] = sums


def factor_kernel(h, c, cm, ids, lam_ref, r_ref, q_ref, d_ref, w_ref, pu, pd, au, ad, al):
    b = ids[2]
    lam = lam_ref[...]
    one = jnp.ones((KB, NY), F32)

    def up_block(bb, alpha):
        au[bb] = alpha

        def step(i, carry):
            n, d, pr = carry
            z = bb * BL + i
            e = n + cm[z] * d
            return (lam * h[z]) * e + n * cm[z], e, pr * cm[z]

        n, d, pr = lax.fori_loop(0, BL, step, (alpha, one, F32(1.0)), unroll=4)
        inv = 1.0 / d
        pu[bb] = pr * inv
        return n * inv

    lax.fori_loop(0, 8, up_block, one)

    def dn_block(j, beta):
        bb = 7 - j
        ad[bb] = beta
        first = jnp.where(j == 0, 0.0, 1.0)

        def step(i, carry):
            n, d, pr = carry
            z = bb * BL + BL - 1 - i
            e = n + c[z] * d
            return (lam * h[z]) * e + n * c[z], e, pr * c[z]

        n, d, pr = lax.fori_loop(0, BL, step, (beta, one * first, first), unroll=4)
        inv = 1.0 / d
        pd[bb] = pr * inv
        return n * inv

    lax.fori_loop(0, 8, dn_block, one)

    def own_up(i, alpha):
        z = b * BL + i
        r = cm[z] / (alpha + cm[z])
        alpha = lam * h[z] + alpha * r
        r_ref[i] = r
        al[i] = alpha
        return alpha

    lax.fori_loop(0, BL, own_up, au[b])

    def own_dn(j, beta):
        i = BL - 1 - j
        z = b * BL + i
        keep = jnp.where(jnp.logical_and(b == 7, j == 0), 0.0, 1.0)
        inv = c[z] / (beta + c[z] * keep)
        through = beta * inv
        q_ref[i] = inv * keep
        d_ref[i] = (1.0 / (NX * NY)) / (al[i] + through)
        return lam * h[z] + through

    lax.fori_loop(0, BL, own_dn, ad[b])
    quad = (b // 4) * 4
    w_ref[0] = pu[b | 1]
    w_ref[1] = pd[(b // 2) * 2]
    w_ref[2] = pu[quad + 2] * pu[quad + 3]
    w_ref[3] = pd[quad] * pd[quad + 1]

    def chosen(flag, value):
        return jnp.where(jnp.full((KB, NY), flag.astype(jnp.int32)) > 0, value, one)

    def ahead(span, upper, inner):
        value = one
        for k in range(1, span):
            climb = jnp.logical_and(upper, inner >= k)
            fall = jnp.logical_and(jnp.logical_not(upper), inner + k < span)
            value = value * chosen(climb, pu[jnp.maximum(b - k, 0)]) * chosen(fall, pd[jnp.minimum(b + k, 7)])
        return value

    w_ref[4] = ahead(2, ((b // 2) & 1) == 1, b & 1)
    w_ref[5] = ahead(4, b >= 4, b & 3)


def sweep_kernel(h, ids, tab, thrust, col_ref, o_ref, r_ref, q_ref, rhs_ref, st_ref, f_ref):
    b, dom = ids[2], ids[5]
    sums = col_ref[0, 2 * KB :]
    for j in range(1, 8):
        sums = sums + col_ref[j, 2 * KB :]
    total = jnp.sum(sums, axis=1, keepdims=True)
    for i in range(BL):
        rhs_ref[i] = col_ref[i // 2, (i % 2) * KB : (i % 2 + 1) * KB]
    for t in range(NT):
        count = ((tab[dom, t, 2] - tab[dom, t, 1]) * (tab[dom, t, 4] - tab[dom, t, 3])).astype(F32)
        strength = jnp.where(dom > 0, thrust[dom, t], 0.0)
        speed = total[t : t + 1] / jnp.full((1, 1), count, F32)
        force = strength * speed * jnp.abs(speed)
        f_ref[t : t + 1] = jnp.broadcast_to(force, (1, 128))
        za, ze = tab[dom, t, 3] - b * BL, tab[dom, t, 4] - b * BL

        def add(i, _):
            rhs_ref[i] = rhs_ref[i] + force * o_ref[t]
            return 0

        lax.fori_loop(jnp.clip(za, 0, BL), jnp.clip(ze, 0, BL), add, 0)

    carry = jnp.zeros((KB, NY), F32)
    for i in range(BL):
        v = rhs_ref[i] * (-h[b * BL + i])
        rhs_ref[i] = v
        carry = v + r_ref[i] * carry
    st_ref[0] = carry
    carry = jnp.zeros((KB, NY), F32)
    for i in reversed(range(BL)):
        carry = rhs_ref[i] + q_ref[i] * carry
    st_ref[1] = carry


def solve_kernel(rhs_ref, r_ref, q_ref, d_ref, i_ref, j_ref, out_ref):
    f = i_ref[...]
    for i in range(BL):
        f = rhs_ref[i] + r_ref[i] * f
        out_ref[i] = f
    g = j_ref[...]
    for i in reversed(range(BL)):
        g = rhs_ref[i] + q_ref[i] * g
        out_ref[i] = (out_ref[i] + (g - rhs_ref[i])) * d_ref[i]


def body(
    velocity, eddy_viscosity, cell_height, z_vectors, z_inverse, z_values,
    feed_source, fringe_strength, fringe_start, turbines, thrust,
):
    u = velocity[0]
    yi, zhi, zb = lax.axis_index("y"), lax.axis_index("zh"), lax.axis_index("zb")
    lane_id = lax.axis_index(XC)
    slab = lax.axis_index(G)
    dom = yi * 2 + zhi
    ids = jnp.stack([yi, zhi, zb, lane_id, slab, dom, slab * 2, slab * 0]).astype(jnp.int32)
    up_perm = [(k, k + 1) for k in range(63)]
    dn_perm = [(k + 1, k) for k in range(63)]
    x0 = fringe_start[0]
    barrier = lax.optimization_barrier

    main = lax.dynamic_slice(u, (0, 0, x0, 0), (3, 2, FR, NY)).reshape(6 * FR, NY)
    left = lax.dynamic_slice(u, (0, 0, (x0 + NX - 1) % NX, 0), (3, 2, 1, NY)).reshape(6, NY)
    right = lax.dynamic_slice(u, (0, 0, (x0 + FR) % NX, 0), (3, 2, 1, NY)).reshape(6, NY)
    raw = jnp.concatenate([main, left, right, jnp.zeros((4, NY), BF16)], 0)
    other = lax.ppermute(raw, "zh", [(0, 1), (1, 0)])
    around = lambda v, s: lax.ppermute(v, "y", [(k, (k + s) % 4) for k in range(4)])
    below = lax.ppermute(jnp.concatenate([u[:, 1], u[2:3, 0]], 0), G, up_perm)
    above = lax.ppermute(u[:, 0], G, dn_perm)
    ring = [around(raw, 3), around(raw, 2), around(raw, 1)]

    cas = jnp.asarray(CAS)
    odd = jnp.asarray(ODD)
    odd_t = jnp.asarray(ODD_T)
    weights = call(
        weights_kernel, sds((3, 3, FR, 128)),
        ids, feed_source, fringe_strength, jnp.asarray(PROFILE),
        specs=[SM, SM, SM, VM],
        scratch=[pltpu.VMEM((24, FR, 128), F32)] * 2,
        name="weights",
    )
    place = jnp.arange(NX, dtype=jnp.int32)
    mode = jnp.where(place < NX // 2, 2 * place, 2 * place - NX + 1)
    planes = jnp.minimum(jnp.arange(48, dtype=jnp.int32), FR + 8) + x0
    angle = 2.0 * jnp.pi / NX * ((mode[:, None] * planes[None, :]) % NX).astype(F32)
    rows = jnp.cos(angle) + jnp.sin(angle)

    diff, spec_main, lines = call(
        main_kernel, (sds((3, 2, NX, NY)), sds((2, NX, NY)), sds((2, NT, NY))),
        cell_height, eddy_viscosity, ids, turbines, u, below, above, cas, odd,
        specs=[SM] * 4 + [VM] * 5,
        scratch=[pltpu.VMEM((13, NX, NY), F32), pltpu.VMEM((2, NX, NY), F32), pltpu.VMEM((NX, NY), F32)],
        name="main",
    )

    other, _ = barrier((other, spec_main))
    far = [around(other, 3), around(other, 2), around(other, 1)]
    raws = [raw, other]
    for near, distant in zip(ring, far):
        raws += [near, distant]
    loc, vup_s, vdn_s, part = call(
        combine_kernel, (sds((6, FR, NY)), sds((5, FR, NY)), sds((3, FR, NY)), sds((NT, NY))),
        cell_height, eddy_viscosity, ids, turbines, fringe_start, weights, lines, *raws,
        specs=[SM] * 5 + [VM] * 10,
        name="combine",
    )
    vup = lax.ppermute(vup_s, G, up_perm)
    vdn = lax.ppermute(vdn_s, G, dn_perm)
    p_up = lax.ppermute(part, "zb", [(k, k + 1) for k in range(7)])
    p_dn = lax.ppermute(part, "zb", [(k + 1, k) for k in range(7)])
    packet, delta = call(
        correct_kernel, (sds((8, 2 * KB + NT, NY)), sds((6, FR, NY))),
        cell_height, eddy_viscosity, ids, loc, vup, vdn, vdn_s, part, p_up, p_dn, spec_main, rows[:, :40], cas,
        specs=[SM] * 3 + [VM] * 10,
        name="correct",
    )
    columns = lax.all_to_all(packet, XC, 0, 0, tiled=True)

    next_height = jnp.concatenate([cell_height[1:], jnp.zeros((1,), F32)])
    coupling = 1.0 / (0.5 * (cell_height + next_height))
    coupling_below = jnp.concatenate([jnp.zeros((1,), F32), coupling[:-1]])
    k_own = lax.dynamic_slice_in_dim(mode, lane_id * KB, KB, 0)
    lam = wave_term(k_own, NX)[:, None] + wave_term(jnp.arange(NY, dtype=jnp.int32), NY)[None, :]
    table = lax.dynamic_index_in_dim(turbines, dom, 0, keepdims=False)
    turn = lambda col: 2.0 * jnp.pi / NX * ((col[:, None] * k_own[None, :]) % NX).astype(F32)
    wave = lambda a: jnp.cos(a) + jnp.sin(a)
    ax = wave(turn(table[:, 0] + 1)) - wave(turn(table[:, 0]))
    span_y = jnp.arange(NY, dtype=jnp.int32)[None, :]
    cells_y = ((span_y >= table[:, 1:2]) & (span_y < table[:, 2:3])).astype(F32)
    cas32 = cas[0].astype(F32) + cas[1].astype(F32)
    by = jnp.dot(cells_y, cas32, precision=HIGHEST)
    outer = ax[:, :, None] * by[:, None, :]
    plane = (KB, NY)
    lam, _ = barrier((lam, packet))
    r, q, inv_den, w = call(
        factor_kernel,
        (sds((BL, *plane)), sds((BL, *plane)), sds((BL, *plane)), sds((6, *plane))),
        cell_height, coupling, coupling_below, ids, lam,
        specs=[SM, SM, SM, SM, VM],
        scratch=[pltpu.VMEM((8, *plane), F32)] * 4 + [pltpu.VMEM((BL, *plane), F32)],
        name="factors",
    )

    rhs, mine, force = call(
        sweep_kernel, (sds((BL, *plane)), sds((2, *plane)), sds((NT, 128))),
        cell_height, ids, turbines, thrust, columns, outer, r, q,
        specs=[SM] * 4 + [VM] * 4,
        name="sweep",
    )
    flow = pl.pallas_call(
        blend_kernel, out_shape=sds((3, 2, NX, NY)), in_specs=[SM] * 3 + [VM] * 3, out_specs=VM,
        input_output_aliases={5: 0}, name="blend",
    )(ids, fringe_start, turbines, delta, force, diff)

    swap = lambda v, k: lax.ppermute(v, "zb", [(j, j ^ k) for j in range(8)])
    zero = jnp.zeros(plane, F32)
    upper = (zb & 1) == 1
    got = swap(mine, 1)
    a = jnp.where(upper, got[0], zero)
    e = jnp.where(upper, zero, got[1])
    merged = jnp.stack([
        jnp.where(upper, mine[0], got[0]) + w[0] * jnp.where(upper, got[0], mine[0]),
        jnp.where(upper, got[1], mine[1]) + w[1] * jnp.where(upper, mine[1], got[1]),
    ])
    upper = (zb & 2) == 2
    got = swap(merged, 2)
    a = a + jnp.where(upper, w[4] * got[0], zero)
    e = e + jnp.where(upper, zero, w[4] * got[1])
    total = jnp.where(
        zb >= 4,
        jnp.where(upper, got[1], merged[1]) + w[3] * jnp.where(upper, merged[1], got[1]),
        jnp.where(upper, merged[0], got[0]) + w[2] * jnp.where(upper, got[0], merged[0]),
    )
    got = swap(total, 4)
    a = a + jnp.where(zb >= 4, w[5] * got, zero)
    e = e + jnp.where(zb >= 4, zero, w[5] * got)
    (a, e), flow = barrier(((a, e), flow))
    solved = call(
        solve_kernel, sds((BL, *plane)), rhs, r, q, inv_den, a, e, specs=[VM] * 6, name="solve"
    )
    returned = lax.all_to_all(solved.reshape(8, 2 * KB, NY), XC, 0, 0, tiled=True)

    p0 = call(first_kernel, sds((NX, NY)), returned, cas, odd_t, specs=[VM] * 3, name="first")
    p2 = lax.ppermute(p0, G, dn_perm)
    partial, p1 = call(
        final_kernel, (sds((1, 3, 2, NX, NY), BF16), sds((NX, NY))),
        cell_height, ids, returned, p0, flow, cas, odd_t,
        specs=[SM] * 2 + [VM] * 5,
        name="final",
    )
    one = lambda *shape: pl.BlockSpec(shape, lambda i: tuple(2 if k == len(shape) - 4 else 1 if k == len(shape) - 3 else 0 for k in range(len(shape))))
    whole = pl.BlockSpec((NX, NY), lambda i: (0, 0))
    return pl.pallas_call(
        top_kernel, grid=(1,), out_shape=sds((1, 3, 2, NX, NY), BF16),
        in_specs=[SM, SM, pl.BlockSpec(memory_space=pl.ANY), whole, whole, one(1, 1, NX, NY)],
        out_specs=one(1, 1, 1, NX, NY),
        input_output_aliases={2: 0}, name="top",
    )(cell_height, ids, partial, p1, p2, flow)


def solution(mesh):
    fine = Mesh(mesh.devices.reshape(4, 2, 8, 4, 2), ("y", "zh", "zb", "x", "c"))
    spec = P(("y", "zh"), None, ("zb", "x", "c"), None, None)
    return jax.shard_map(
        body, mesh=fine, in_specs=(spec,) + (P(),) * 10, out_specs=spec, check_vma=False
    )
```
